32 devices in a mesh: prow: 16 (over z, y, x), pcol: 2 (over core).
Axes of the slice: x: 2, y: 2, z: 4, core: 2. Of those that a mesh axis runs over, the one named last changes fastest.
Arguments:
- right_sides: float32 [32, 1, 4096], P(None, None, 'prow'), may hold values from -6 to 6
- factor: bfloat16 [1, 4096, 8, 512], P(None, 'prow', None, 'pcol'), as said below
- node_sizes: int32 [7], replicated, may hold values from 1 to 9, 16 in all
- row_blocks: int32 [7, 16], replicated, may hold values 0 or 1
Outputs:
- forward: float32 [32, 1, 4096], P(None, None, 'prow')
- solution: float32 [32, 8, 512], P(None, None, 'pcol')
The draws below stay inside these ranges and needn't reach their ends.
Inputs may be any that keep to these rules, and one draw needn't show every extreme that they name: factor is zero above its diagonal; its diagonal lies between 0.5 and 1. `row_blocks`: flags of tiles that belong to no proper ancestor of the supernode are ignored.
All inputs are finite; a program needn't handle non-finite values.
Results may differ from the reference program's by a relative error of at most 0.0047.
Values may be sent and summed in bfloat16 or wider, within the bound.
A program may use at most 64 MiB of HBM per device.

```python
import math
import jax
import jax.numpy as jnp
import numpy as np
from jax import lax

B = 256
RHS = 32
LEVELS = 3
RT = 1
SN = 7
NT = 16
CT = 8
WMAX = 9
N_PROW = 16
N_PCOL = 2


def draw_factor(key, part):
    order_len = NT * B
    key_off, key_diag = jax.random.split(key, 2)

    def one_block(block_id):
        block_key = jax.random.fold_in(key_off, block_id)
        diag_key = jax.random.fold_in(key_diag, block_id)
        spread = jax.random.truncated_normal(block_key, -4.0, 4.0, (B, order_len), jnp.float32)
        spread = spread * (1.5 / order_len ** 0.5)
        diag_vals = jax.random.uniform(diag_key, (B,), jnp.float32, 0.5, 1.0)
        row_ids = block_id * B + jnp.arange(B, dtype=jnp.int32)
        col_ids = jnp.arange(order_len, dtype=jnp.int32)
        values = jnp.where(col_ids[None, :] > row_ids[:, None], 0.0, spread)
        values = jnp.where(col_ids[None, :] == row_ids[:, None], diag_vals[:, None], values)
        return values
    blocks = lax.map(one_block, jnp.arange(NT, dtype=jnp.int32))
    return blocks.reshape(RT, order_len // RT, CT, order_len // CT).astype(jnp.bfloat16)


def touch_ends(array, rng, least, largest):
    longest = array.shape.index(max(array.shape))
    spots = []
    for shift in (0, 1):
        where = [jax.random.randint(jax.random.fold_in(rng, axis), (), 0, length) for axis, length in enumerate(array.shape)]
        where[longest] = (where[longest] + shift) % array.shape[longest]
        spots.append(tuple(where))
    return array.at[spots[0]].set(least).at[spots[1]].set(largest)


def levels(stream_key, extent, cuts, low, top_value):
    def one(position, shards_of):
        draws = jax.random.uniform(jax.random.fold_in(jax.random.fold_in(stream_key, 6), position), (shards_of,), jnp.float32, low / len(cuts), top_value / len(cuts))
        return jnp.repeat(jnp.exp(draws), extent[position] // shards_of).reshape((-1,) + (1,) * (len(extent) - position - 1))

    gain = one(*cuts[0])
    for cut in cuts[1:]:
        gain = gain * one(*cut)
    return gain


def profile(amount, total, bound, lean):
    weights = [(1 << 20) // math.isqrt(rank ** lean) + 1 for rank in range(2, amount + 1)]
    spare, holding = total - bound - (amount - 1), [1] * (amount - 1)
    while spare > 0:
        free = [i for i in range(amount - 1) if holding[i] < bound]
        mass, left = sum([weights[i] for i in free]), spare
        for i in free:
            more = min(bound - holding[i], max(1, left * weights[i] // mass), spare)
            holding[i] = holding[i] + more
            spare = spare - more
    return np.array([bound] + holding)


def uneven(own_key, amount, total, reach, skew):
    if amount == 2:
        one = jax.random.randint(own_key, (), max(1, total - reach), min(reach, total - 1) + 1)
        return jnp.stack([one, total - one])
    sizes = jnp.asarray(profile(amount, total, reach, skew), jnp.int32)
    couples = (amount - 1) // 2
    donor, taker = sizes[1:1 + 2 * couples:2], sizes[2:2 + 2 * couples:2]
    margin = jnp.minimum(donor - 1, reach - taker)
    passed = jax.random.randint(jax.random.fold_in(own_key, 1), (couples,), 0, 1 << 20) % (margin + 1)
    sizes = sizes.at[1:1 + 2 * couples:2].set(donor - passed).at[2:2 + 2 * couples:2].set(taker + passed)
    return sizes[jax.random.permutation(jax.random.fold_in(own_key, 2), amount)]


def centred(rng, shape, scale, limit, pieces=(), held_as=jnp.bfloat16):
    drawn = jax.random.normal(rng, shape, jnp.float32) * scale
    if len(pieces) > 0:
        drawn = levels(rng, shape, pieces, -0.22, 0.18) * drawn
    return jnp.clip(drawn, min=-limit, max=limit).astype(held_as)


def setup_inputs(seed: int = 0) -> dict:
    seeds = jax.random.split(jax.random.key(seed), 5)
    return {
        "right_sides": centred(seeds[0], (RHS, RT, N_PROW * B), 1.0, 6.0, ((2, 16),), jnp.float32),
        "factor": draw_factor(jax.random.fold_in(seeds[4], 71), 0),
        "node_sizes": uneven(seeds[2], SN, NT, WMAX, 1).astype(jnp.int32),
        "row_blocks": touch_ends((jax.random.randint(seeds[3], (SN, NT), 0, 2) < 1).astype(jnp.int32), jax.random.fold_in(seeds[3], 1), 0, 1),
    }


def tree_tables(node_sizes, row_blocks):
    node_count = node_sizes.shape[0]
    tile_count = row_blocks.shape[1]
    tile_ends = jnp.cumsum(node_sizes).astype(jnp.int32)
    tile_starts = (tile_ends - node_sizes).astype(jnp.int32)
    tile_ids = jnp.arange(tile_count, dtype=jnp.int32)
    node_of = jnp.sum((tile_ends[None, :] <= tile_ids[:, None]).astype(jnp.int32), axis=1).astype(jnp.int32)
    heap_label = (node_count - jnp.arange(node_count, dtype=jnp.int32)).astype(jnp.int32)
    node_depth = jnp.zeros((node_count,), jnp.int32)
    for exponent in range(1, LEVELS):
        node_depth = node_depth + (heap_label >= 2 ** exponent).astype(jnp.int32)
    gap_depth = jnp.maximum(node_depth[None, :] - node_depth[:, None], 0).astype(jnp.int32)
    ancestor = (node_depth[:, None] < node_depth[None, :]) & (jnp.right_shift(heap_label[None, :], gap_depth) == heap_label[:, None])
    return tile_starts, node_of, ancestor


def reference(right_sides, factor, node_sizes, row_blocks):
    full_order = NT * B
    window_len = WMAX * B
    matrix = factor.reshape(full_order, full_order)
    tile_starts, node_of, ancestor = tree_tables(node_sizes, row_blocks)
    linked = ancestor[node_of][:, node_of] & (row_blocks[node_of, :].T == 1)

    def window_of(tile_id):
        window_start = jnp.minimum(tile_starts[node_of[tile_id]] * B, full_order - window_len).astype(jnp.int32)
        positions = window_start + jnp.arange(window_len, dtype=jnp.int32)
        inside = node_of[positions // B] == node_of[tile_id]
        return window_start, inside

    def forward_step(counter, loop_state):
        residual, solved = loop_state
        tile_id = jnp.asarray(counter).astype(jnp.int32)
        window_start, inside = window_of(tile_id)
        diag_rows = lax.dynamic_slice(matrix, (tile_id * B, window_start), (B, window_len))
        segment = lax.dynamic_slice(residual, (jnp.int32(0), window_start), (RHS, window_len))
        segment = jnp.where(inside[None, :], segment, 0.0).astype(jnp.bfloat16)
        answer = jnp.dot(segment, diag_rows.T, preferred_element_type=jnp.float32)
        solved = lax.dynamic_update_slice(solved, answer, (jnp.int32(0), tile_id * B))
        column = lax.dynamic_slice(matrix, (jnp.int32(0), tile_id * B), (full_order, B))
        rows_on = jnp.repeat(linked[:, tile_id], B)
        product = jnp.dot(answer.astype(jnp.bfloat16), column.T, preferred_element_type=jnp.float32)
        residual = residual - jnp.where(rows_on[None, :], product, 0.0)
        return residual, solved

    start_state = (right_sides.reshape(RHS, full_order).astype(jnp.float32), jnp.zeros((RHS, full_order), jnp.float32))
    residual, forward = lax.fori_loop(0, NT, forward_step, start_state)

    def backward_step(counter, loop_state):
        residual, solved = loop_state
        tile_id = (NT - 1 - jnp.asarray(counter)).astype(jnp.int32)
        window_start, inside = window_of(tile_id)
        diag_cols = lax.dynamic_slice(matrix, (window_start, tile_id * B), (window_len, B))
        segment = lax.dynamic_slice(residual, (jnp.int32(0), window_start), (RHS, window_len))
        segment = jnp.where(inside[None, :], segment, 0.0).astype(jnp.bfloat16)
        answer = jnp.dot(segment, diag_cols, preferred_element_type=jnp.float32)
        solved = lax.dynamic_update_slice(solved, answer, (jnp.int32(0), tile_id * B))
        row_slab = lax.dynamic_slice(matrix, (tile_id * B, jnp.int32(0)), (B, full_order))
        cols_on = jnp.repeat(linked[tile_id, :], B)
        product = jnp.dot(answer.astype(jnp.bfloat16), row_slab, preferred_element_type=jnp.float32)
        residual = residual - jnp.where(cols_on[None, :], product, 0.0)
        return residual, solved

    rounded = lax.optimization_barrier(forward.astype(jnp.bfloat16))
    back_state = (rounded.astype(jnp.float32), jnp.zeros((RHS, full_order), jnp.float32))
    residual, solution = lax.fori_loop(0, NT, backward_step, back_state)
    return forward.reshape(RHS, RT, N_PROW * B), solution.reshape(RHS, CT, N_PCOL * B)
```

```python
import functools

import jax
import jax.numpy as jnp
from jax import lax
from jax.experimental import pallas as pl
from jax.experimental.pallas import tpu as pltpu
from jax.sharding import PartitionSpec as P

MESH = pl.DeviceIdType.MESH
NT_DIMS = (((1,), (1,)), ((), ()))
NN_DIMS = (((1,), (0,)), ((), ()))
GATHER = 2
SPLIT = 2
CHUNK = 64
LANES = 128
PACK = 16


def kernel(
    R, C, CT, LEVELS, H,
    sizes_ref, blocks_ref, b_ref, factor_ref,
    fwd_ref, sol_ref,
    raw, wide, a_ref,
    ag_src, ag_buf, rs_src, rs_buf, fwd_buf, fin_src, fin_buf,
    ag_send, ag_recv, rs_send, rs_recv,
    fwd_send, fwd_recv, fin_send, fin_recv, raw_send, raw_recv, load_sem,
):
    SN = sizes_ref.shape[0]
    me = lax.axis_index("prow")
    col = lax.axis_index("pcol")
    base = (col // H) * H
    g = lax.rem(col, H)
    T = b_ref.shape[2]
    Q = b_ref.shape[0] // H
    f32, bf16 = jnp.float32, jnp.bfloat16

    widest = R - SN + 1
    lows, highs = [], []
    for level in range(LEVELS):
        first = SN - 1 - (2 ** (level + 1) - 2)
        last = SN - 1 - (2**level - 1)
        lows.append(first)
        highs.append(R - SN + last)

    load = pltpu.make_async_copy(factor_ref.at[0], raw.at[col], load_sem)
    load.start()
    barrier = pltpu.get_barrier_semaphore()

    def greet(step, carry):
        row = lax.rem(me + R - 1 - step, R)
        for j in range(H):
            @pl.when(jnp.logical_or(step < R - 1, j > 0))
            def _():
                pl.semaphore_signal(
                    barrier, inc=1, device_id=(row, base + lax.rem(g + j, H)),
                    device_id_type=MESH,
                )
        return carry

    lax.fori_loop(0, R, greet, 0)

    def greet_row(step, carry):
        pl.semaphore_signal(
            barrier, inc=1, device_id=(me, lax.rem(base + H + step, C)),
            device_id_type=MESH,
        )
        return carry

    lax.fori_loop(0, C - H, greet_row, 0)

    ends = []
    total = jnp.int32(0)
    for s in range(SN):
        total = total + sizes_ref[s]
        ends.append(total)

    def node_of(tile):
        count = jnp.int32(0)
        for s in range(SN):
            count = count + jnp.where(ends[s] <= tile, 1, 0)
        return jnp.minimum(count, SN - 1)

    def level_of(label):
        level = jnp.int32(0)
        for e in range(1, LEVELS):
            level = level + jnp.where(label >= 2**e, 1, 0)
        return level

    row_node = node_of(me)
    row_label = SN - row_node
    row_level = level_of(row_label)
    same, linked, tile_level = [], [], []
    for k in range(R):
        node = node_of(k)
        label = SN - node
        above = jnp.int32(0)
        for gap in range(1, LEVELS):
            above = above + jnp.where(jnp.right_shift(label, gap) == row_label, 1, 0)
        flag = jnp.where(blocks_ref[node, me] == 1, 1, 0)
        low = jnp.where(k <= me, 1, 0)
        same.append(jnp.where(node == row_node, 1, 0) * low)
        linked.append(above * flag * low)
        tile_level.append(level_of(label))

    def inner(level):
        here = jnp.where(row_level == level, 1, 0)
        return [same[k] * here > 0 for k in range(R)]

    def outer(level):
        return [
            linked[k] * jnp.where(tile_level[k] == level, 1, 0) > 0 for k in range(R)
        ]

    b = b_ref[pl.ds(pl.multiple_of(g * Q, Q), Q), 0, :]
    zeros = jnp.zeros((Q, T), f32)

    def relayout(c):
        def body(step, carry):
            start = pl.multiple_of(step * CHUNK, CHUNK)
            rows = pl.ds(start, CHUNK)
            for h in range(T // LANES):
                block = raw[c, rows, :, h * LANES:(h + 1) * LANES].astype(f32)
                wide[h] = block.reshape(CHUNK * CT, LANES)
            for s in range(CT):
                for h in range(T // LANES):
                    part = wide[h, pl.ds(s, CHUNK, stride=CT), :]
                    at = pl.multiple_of((s * C + c) * T + h * LANES, LANES)
                    a_ref[rows, pl.ds(at, LANES)] = part.astype(bf16)
            return carry

        lax.fori_loop(0, T // CHUNK, body, 0)

    load.wait()
    relayout(col)
    pl.semaphore_wait(barrier, R * H - 1 + C - H)

    def raw_copy(step):
        return pltpu.make_async_remote_copy(
            src_ref=factor_ref.at[0], dst_ref=raw.at[col],
            send_sem=raw_send.at[step], recv_sem=raw_recv.at[col],
            device_id=(me, lax.rem(col + step, C)), device_id_type=MESH,
        )

    def raw_arrive(step, carry):
        origin = lax.rem(col + step, C)
        pltpu.make_async_remote_copy(
            src_ref=factor_ref.at[0], dst_ref=raw.at[origin],
            send_sem=raw_send.at[step], recv_sem=raw_recv.at[origin],
            device_id=(me, origin), device_id_type=MESH,
        ).wait_recv()
        relayout(origin)
        return carry

    def ag_copy(rnd, k):
        return pltpu.make_async_remote_copy(
            src_ref=ag_src.at[rnd], dst_ref=ag_buf.at[rnd, me],
            send_sem=ag_send.at[rnd, k], recv_sem=ag_recv.at[rnd, me],
            device_id=(k, col), device_id_type=MESH,
        )

    def forward_range(level, far):
        if far:
            first, last, reach = lows[level - 1], R - 1, R
        else:
            first, last, reach = lows[level], highs[level], widest - 1
        active = jnp.logical_and(me >= lows[level], me <= highs[level])
        start = jnp.maximum(me + 1, first)
        stop = jnp.minimum(me + reach, last) + 1
        return start, jnp.where(active, jnp.maximum(stop, start), start)

    def send_row(rnd, level, far, value):
        start, stop = forward_range(level, far)
        ag_src[rnd] = value
        lax.fori_loop(
            0, stop - start, lambda i, x: (ag_copy(rnd, stop - 1 - i).start(), x)[1], 0
        )
        ag_buf[rnd, me] = value

    def sent_row(rnd, level, far):
        start, stop = forward_range(level, far)
        lax.fori_loop(start, stop, lambda k, x: (ag_copy(rnd, k).wait_send(), x)[1], 0)

    def row_arrive(rnd, k):
        pltpu.make_async_remote_copy(
            src_ref=ag_src.at[rnd], dst_ref=ag_buf.at[rnd, k],
            send_sem=ag_send.at[rnd, k], recv_sem=ag_recv.at[rnd, k],
            device_id=(me, col), device_id_type=MESH,
        ).wait_recv()

    def multiply(rnd, level, far, masks):
        lo, hi = lows[level], highs[level]
        zero = jnp.zeros((Q, T), bf16)
        out = None
        for last in range(hi + 1, lo, -GATHER):
            group = range(max(last - GATHER, lo), last)
            for k in reversed(group):
                if far:
                    due = jnp.logical_and(me > k, me >= lows[level - 1])
                else:
                    due = jnp.logical_and(me > k, me <= min(hi, k + widest - 1))
                pl.when(due)(functools.partial(row_arrive, rnd, k))
            parts = [jnp.where(masks[k], ag_buf[rnd, k], zero) for k in group]
            value = lax.dot_general(
                jnp.concatenate(parts, axis=1), a_ref[:, group[0] * T:last * T], NT_DIMS,
                preferred_element_type=f32,
            )
            out = value if out is None else out + value
        return out

    forward = zeros
    correction = zeros
    rnd = 0
    before = None
    for level in range(LEVELS - 1, -1, -1):
        send_row(rnd, level, False, (b - correction).astype(bf16))
        if rnd == 0:
            for step in range(1, C):
                raw_copy(step).start()
            lax.fori_loop(1, C, raw_arrive, 0)
        if before is not None:
            sent_row(*before)
        before = (rnd, level, False)
        solved = multiply(rnd, level, False, inner(level))
        solved = jnp.where(row_level == level, solved, zeros)
        forward = forward + solved
        rnd += 1
        if level > 0:
            send_row(rnd, level, True, solved.astype(bf16))
            sent_row(*before)
            before = (rnd, level, True)
            correction = correction + multiply(rnd, level, True, outer(level))
            rnd += 1
    rounded = forward.astype(bf16)
    start_value = rounded.astype(f32)

    def rs_copy(rnd, t):
        return pltpu.make_async_remote_copy(
            src_ref=rs_src.at[rnd, t], dst_ref=rs_buf.at[rnd, me],
            send_sem=rs_send.at[rnd, t], recv_sem=rs_recv.at[rnd, me],
            device_id=(t, col), device_id_type=MESH,
        )

    def goes(level, far, t):
        if far:
            return jnp.logical_and(me > t, me >= lows[level - 1])
        return jnp.logical_and(me > t, me <= min(highs[level], t + widest - 1))

    def scatter(rnd, level, far, value, masks):
        lo, hi = lows[level], highs[level]
        for first in range(lo, hi + 1, SPLIT):
            group = range(first, min(first + SPLIT, hi + 1))
            blocks = lax.dot_general(
                value, a_ref[:, group[0] * T:(group[-1] + 1) * T], NN_DIMS,
                preferred_element_type=f32,
            )
            for i, t in enumerate(group):
                rs_src[rnd, t] = jnp.where(
                    masks[t], blocks[:, i * T:(i + 1) * T], zeros
                ).astype(bf16)
                pl.when(goes(level, far, t))(rs_copy(rnd, t).start)

    def scattered(rnd, level, far):
        for t in range(lows[level], highs[level] + 1):
            pl.when(goes(level, far, t))(rs_copy(rnd, t).wait_send)

    def reduce(rnd, level, far, out):
        def arrive(k, carry):
            pltpu.make_async_remote_copy(
                src_ref=rs_src.at[rnd, 0], dst_ref=rs_buf.at[rnd, k],
                send_sem=rs_send.at[rnd, 0], recv_sem=rs_recv.at[rnd, k],
                device_id=(k, col), device_id_type=MESH,
            ).wait_recv()
            return carry + rs_buf[rnd, k].astype(f32)

        active = jnp.logical_and(me >= lows[level], me <= highs[level])
        if far:
            start, last = jnp.maximum(me + 1, lows[level - 1]), jnp.int32(R - 1)
        else:
            start = me + 1
            last = jnp.minimum(me + widest - 1, highs[level])
        stop = jnp.where(active, jnp.maximum(last + 1, start), start)
        return lax.fori_loop(start, stop, arrive, out)

    def fin_copy(row):
        return pltpu.make_async_remote_copy(
            src_ref=fin_src, dst_ref=fin_buf.at[me // C, g],
            send_sem=fin_send.at[row], recv_sem=fin_recv.at[me // C, g],
            device_id=(row, lax.rem(me, C)), device_id_type=MESH,
        )

    giver = lax.rem(me, C) // H == col // H
    local = lax.rem(me, C) == col

    def give(value):
        fin_src[...] = value.astype(bf16)

        def one(step, carry):
            fin_copy(lax.rem(me + step, R)).start()
            return carry

        lax.fori_loop(1, R, one, 0)

        @pl.when(local)
        def _():
            fin_buf[me // C, g] = value.astype(bf16)

        @pl.when(jnp.logical_not(local))
        def _():
            fin_copy(me).start()

    def fwd_copy(j):
        return pltpu.make_async_remote_copy(
            src_ref=fwd_buf.at[g], dst_ref=fwd_buf.at[g],
            send_sem=fwd_send.at[j], recv_sem=fwd_recv.at[g],
            device_id=(me, base + lax.rem(g + j, H)), device_id_type=MESH,
        )

    answer = zeros
    current = rounded
    rnd = 0
    back = None
    for level in range(LEVELS):
        scatter(rnd, level, False, current, inner(level))
        if rnd == 0:
            sent_row(*before)
            fwd_buf[g] = forward
            for j in range(1, H):
                fwd_copy(j).start()
        if back is not None:
            scattered(*back)
        back = (rnd, level, False)
        solved = reduce(rnd, level, False, rs_src[rnd, me].astype(f32))
        answer = answer + jnp.where(row_level == level, solved, zeros)
        top = highs[level + 1] if level + 1 < LEVELS else -1
        ready = jnp.logical_and(me > top, me <= highs[level])

        @pl.when(jnp.logical_and(giver, ready))
        def _():
            give(answer)

        rnd += 1
        if level + 1 < LEVELS:
            scatter(rnd, level + 1, True, answer.astype(bf16), outer(level + 1))
            scattered(*back)
            back = (rnd, level + 1, True)
            current = (start_value - reduce(rnd, level + 1, True, zeros)).astype(bf16)
            rnd += 1
    scattered(*back)

    for step in range(1, C):
        raw_copy(step).wait_send()
    for j in range(1, H):
        fwd_copy(j).wait_send()
    for j in range(1, H):
        other = lax.rem(g + j, H)
        pltpu.make_async_remote_copy(
            src_ref=fwd_buf.at[g], dst_ref=fwd_buf.at[other],
            send_sem=fwd_send.at[j], recv_sem=fwd_recv.at[other],
            device_id=(me, base + other), device_id_type=MESH,
        ).wait_recv()
    for j in range(H):
        fwd_ref[j * Q:(j + 1) * Q, :] = fwd_buf[j]

    def fin_arrive(s, carry):
        for j in range(H):
            @pl.when(jnp.logical_or(s * C + col != me, g != j))
            def _():
                pltpu.make_async_remote_copy(
                    src_ref=fin_src, dst_ref=fin_buf.at[s, j],
                    send_sem=fin_send.at[0], recv_sem=fin_recv.at[s, j],
                    device_id=(me, col), device_id_type=MESH,
                ).wait_recv()
        return carry

    lax.fori_loop(0, CT, fin_arrive, 0)
    for s in range(CT):
        for j in range(H):
            sol_ref[s, j * Q:(j + 1) * Q, :] = fin_buf[s, j]

    @pl.when(giver)
    def _():
        def one(step, carry):
            fin_copy(lax.rem(me + step, R)).wait_send()
            return carry

        lax.fori_loop(1, R, one, 0)

        @pl.when(jnp.logical_not(local))
        def _():
            fin_copy(me).wait_send()


def finish_kernel(rows_ref, tiles_ref, fwd_ref, sol_ref):
    fwd_ref[:, 0, :] = rows_ref[...]
    for s in range(tiles_ref.shape[0]):
        sol_ref[:, s, :] = tiles_ref[s].astype(jnp.float32)


def shards(R, C, right_sides, factor, node_sizes, row_blocks):
    rhs, row_tiles, T = right_sides.shape
    rows, CT = factor.shape[1], factor.shape[2]
    levels = (node_sizes.shape[0] + 1).bit_length() - 1
    assert row_tiles == 1 and rows == T and CT * C == R
    H = min(C, max(rhs // PACK, 1))
    assert C % H == 0 and rhs % H == 0
    Q = rhs // H
    rounds = 2 * levels - 1
    vmem = pl.BlockSpec(memory_space=pltpu.VMEM)
    smem = pl.BlockSpec(memory_space=pltpu.SMEM)
    dma = pltpu.SemaphoreType.DMA
    bf16, f32 = jnp.bfloat16, jnp.float32
    forward, tiles = pl.pallas_call(
        functools.partial(kernel, R, C, CT, levels, H),
        out_shape=(
            jax.ShapeDtypeStruct((rhs, T), f32),
            jax.ShapeDtypeStruct((CT, rhs, T), bf16),
        ),
        in_specs=[smem, smem, vmem, pl.BlockSpec(memory_space=pl.ANY)],
        out_specs=(vmem, vmem),
        scratch_shapes=[
            pltpu.VMEM((C, rows, CT, T), bf16),
            pltpu.VMEM((T // LANES, CHUNK * CT, LANES), f32),
            pltpu.VMEM((rows, R * T), bf16),
            pltpu.VMEM((rounds, Q, T), bf16),
            pltpu.VMEM((rounds, R, Q, T), bf16),
            pltpu.VMEM((rounds, R, Q, T), bf16),
            pltpu.VMEM((rounds, R, Q, T), bf16),
            pltpu.VMEM((H, Q, T), f32),
            pltpu.VMEM((Q, T), bf16),
            pltpu.VMEM((CT, H, Q, T), bf16),
            dma((rounds, R)),
            dma((rounds, R)),
            dma((rounds, R)),
            dma((rounds, R)),
            dma((H,)),
            dma((H,)),
            dma((R,)),
            dma((CT, H)),
            dma((C,)),
            dma((C,)),
            dma,
        ],
        compiler_params=pltpu.CompilerParams(collective_id=0, has_side_effects=True),
        name="tree_solve",
    )(node_sizes, row_blocks, right_sides, factor)

    return pl.pallas_call(
        finish_kernel,
        out_shape=(
            jax.ShapeDtypeStruct((rhs, 1, T), f32),
            jax.ShapeDtypeStruct((rhs, CT, T), f32),
        ),
        in_specs=[vmem, vmem],
        out_specs=(vmem, vmem),
        name="place",
    )(forward, tiles)


def solution(mesh):
    in_specs = (P(None, None, "prow"), P(None, "prow", None, "pcol"), P(), P())
    out_specs = (P(None, None, "prow"), P(None, None, "pcol"))
    body = functools.partial(shards, mesh.shape["prow"], mesh.shape["pcol"])
    return jax.shard_map(
        body, mesh=mesh, in_specs=in_specs, out_specs=out_specs, check_vma=False
    )
```

```python
import functools

import jax
import jax.numpy as jnp
from jax import lax
from jax.experimental import pallas as pl
from jax.experimental.pallas import tpu as pltpu
from jax.sharding import PartitionSpec as P

MESH = pl.DeviceIdType.MESH
NT_DIMS = (((1,), (1,)), ((), ()))
NN_DIMS = (((1,), (0,)), ((), ()))
GATHER = 2
SPLIT = 16
CHUNK = 64
LANES = 128
PACK = 16
GRANT = 32 * 1024 * 1024


def kernel(
    R, C, CT, LEVELS, H,
    sizes_hbm, blocks_hbm, b_hbm, factor_ref,
    fwd_ref, sol_ref,
    sizes_ref, blocks_ref, b_ref,
    raw, wide, a_ref,
    ag_src, ag_buf, rs_src, rs_buf, fwd_buf, fin_src, fin_buf,
    ag_send, ag_recv, rs_send, rs_recv,
    fwd_send, fwd_recv, fin_send, fin_recv, own_sem, raw_send, raw_recv, load_sem, small_sem,
):
    SN = sizes_ref.shape[0]
    me = lax.axis_index("prow")
    col = lax.axis_index("pcol")
    base = (col // H) * H
    g = lax.rem(col, H)
    T = b_ref.shape[2]
    Q = b_ref.shape[0] // H
    f32, bf16 = jnp.float32, jnp.bfloat16

    widest = R - SN + 1
    lows, highs = [], []
    for level in range(LEVELS):
        first = SN - 1 - (2 ** (level + 1) - 2)
        last = SN - 1 - (2**level - 1)
        lows.append(first)
        highs.append(R - SN + last)

    load = pltpu.make_async_copy(factor_ref.at[0], raw.at[col], load_sem)
    small = [
        pltpu.make_async_copy(src, dst, small_sem.at[i])
        for i, (src, dst) in enumerate(
            ((sizes_hbm, sizes_ref), (blocks_hbm, blocks_ref), (b_hbm, b_ref))
        )
    ]
    for copy in small:
        copy.start()
    load.start()
    barrier = pltpu.get_barrier_semaphore()

    def greet(step, carry):
        row = lax.rem(me + R - 1 - step, R)
        for j in range(H):
            @pl.when(jnp.logical_or(step < R - 1, j > 0))
            def _():
                pl.semaphore_signal(
                    barrier, inc=1, device_id=(row, base + lax.rem(g + j, H)),
                    device_id_type=MESH,
                )
        return carry

    lax.fori_loop(0, R, greet, 0)

    def greet_row(step, carry):
        pl.semaphore_signal(
            barrier, inc=1, device_id=(me, lax.rem(base + H + step, C)),
            device_id_type=MESH,
        )
        return carry

    lax.fori_loop(0, C - H, greet_row, 0)

    for copy in small:
        copy.wait()
    ends = []
    total = jnp.int32(0)
    for s in range(SN):
        total = total + sizes_ref[s]
        ends.append(total)

    def node_of(tile):
        count = jnp.int32(0)
        for s in range(SN):
            count = count + jnp.where(ends[s] <= tile, 1, 0)
        return jnp.minimum(count, SN - 1)

    def level_of(label):
        level = jnp.int32(0)
        for e in range(1, LEVELS):
            level = level + jnp.where(label >= 2**e, 1, 0)
        return level

    row_node = node_of(me)
    row_label = SN - row_node
    row_level = level_of(row_label)
    same, linked, tile_level = [], [], []
    for k in range(R):
        node = node_of(k)
        label = SN - node
        above = jnp.int32(0)
        for gap in range(1, LEVELS):
            above = above + jnp.where(jnp.right_shift(label, gap) == row_label, 1, 0)
        flag = jnp.where(blocks_ref[node, me] == 1, 1, 0)
        low = jnp.where(k <= me, 1, 0)
        same.append(jnp.where(node == row_node, 1, 0) * low)
        linked.append(above * flag * low)
        tile_level.append(level_of(label))

    def inner(level):
        here = jnp.where(row_level == level, 1, 0)
        return [same[k] * here > 0 for k in range(R)]

    def outer(level):
        return [
            linked[k] * jnp.where(tile_level[k] == level, 1, 0) > 0 for k in range(R)
        ]

    b = b_ref[pl.ds(pl.multiple_of(g * Q, Q), Q), 0, :]
    zeros = jnp.zeros((Q, T), f32)

    def relayout(c):
        def body(step, carry):
            start = pl.multiple_of(step * CHUNK, CHUNK)
            rows = pl.ds(start, CHUNK)
            for h in range(T // LANES):
                block = raw[c, rows, :, h * LANES:(h + 1) * LANES].astype(f32)
                wide[h] = block.reshape(CHUNK * CT, LANES)
            for s in range(CT):
                for h in range(T // LANES):
                    part = wide[h, pl.ds(s, CHUNK, stride=CT), :]
                    at = pl.multiple_of((s * C + c) * T + h * LANES, LANES)
                    a_ref[rows, pl.ds(at, LANES)] = part.astype(bf16)
            return carry

        lax.fori_loop(0, T // CHUNK, body, 0)

    load.wait()
    relayout(col)
    pl.semaphore_wait(barrier, R * H - 1 + C - H)

    def raw_copy(step):
        return pltpu.make_async_remote_copy(
            src_ref=factor_ref.at[0], dst_ref=raw.at[col],
            send_sem=raw_send.at[step], recv_sem=raw_recv.at[col],
            device_id=(me, lax.rem(col + step, C)), device_id_type=MESH,
        )

    def raw_arrive(step, carry):
        origin = lax.rem(col + step, C)
        pltpu.make_async_remote_copy(
            src_ref=factor_ref.at[0], dst_ref=raw.at[origin],
            send_sem=raw_send.at[step], recv_sem=raw_recv.at[origin],
            device_id=(me, origin), device_id_type=MESH,
        ).wait_recv()
        relayout(origin)
        return carry

    def settle(sem, count, most, sent):
        for n in range(1, most + 1):
            done = pltpu.make_async_remote_copy(
                src_ref=rs_buf.at[0, 0:n], dst_ref=rs_buf.at[0, 0:n],
                send_sem=sem, recv_sem=sem, device_id=(me, col), device_id_type=MESH,
            )
            pl.when(count == n)(done.wait_send if sent else done.wait_recv)

    def ag_copy(rnd, k):
        return pltpu.make_async_remote_copy(
            src_ref=ag_src.at[rnd], dst_ref=ag_buf.at[rnd, me],
            send_sem=ag_send.at[rnd], recv_sem=ag_recv.at[rnd, me // GATHER],
            device_id=(k, col), device_id_type=MESH,
        )

    def forward_range(level, far):
        if far:
            first, last, reach = lows[level - 1], R - 1, R
        else:
            first, last, reach = lows[level], highs[level], widest - 1
        active = jnp.logical_and(me >= lows[level], me <= highs[level])
        start = jnp.maximum(me + 1, first)
        stop = jnp.minimum(me + reach, last) + 1
        return start, jnp.where(active, jnp.maximum(stop, start), start)

    def send_row(rnd, level, far, value):
        start, stop = forward_range(level, far)
        ag_src[rnd] = value
        lax.fori_loop(
            0, stop - start, lambda i, x: (ag_copy(rnd, stop - 1 - i).start(), x)[1], 0
        )
        ag_buf[rnd, me] = value

    def sent_row(rnd, level, far):
        start, stop = forward_range(level, far)
        settle(ag_send.at[rnd], stop - start, R - 1, True)

    def multiply(rnd, level, far, masks):
        lo, hi = lows[level], highs[level]
        zero = jnp.zeros((Q, T), bf16)
        out = None
        for part in range(hi // GATHER, lo // GATHER - 1, -1):
            last = min(part * GATHER + GATHER, hi + 1)
            group = range(max(part * GATHER, lo), last)
            if far:
                first, stop = group[0], jnp.minimum(me, last)
                due = me >= lows[level - 1]
            else:
                first, stop = jnp.maximum(group[0], me - widest + 1), jnp.minimum(me, last)
                due = me <= hi
            count = jnp.where(due, jnp.maximum(stop - first, 0), 0)
            settle(ag_recv.at[rnd, part], count, len(group), False)
            parts = [jnp.where(masks[k], ag_buf[rnd, k], zero) for k in group]
            value = lax.dot_general(
                jnp.concatenate(parts, axis=1), a_ref[:, group[0] * T:last * T], NT_DIMS,
                preferred_element_type=f32,
            )
            out = value if out is None else out + value
        return out

    forward = zeros
    correction = zeros
    rnd = 0
    before = None
    for level in range(LEVELS - 1, -1, -1):
        send_row(rnd, level, False, (b - correction).astype(bf16))
        if rnd == 0:
            for step in range(1, C):
                raw_copy(step).start()
            lax.fori_loop(1, C, raw_arrive, 0)
        if before is not None:
            sent_row(*before)
        before = (rnd, level, False)
        solved = multiply(rnd, level, False, inner(level))
        solved = jnp.where(row_level == level, solved, zeros)
        forward = forward + solved
        rnd += 1
        if level > 0:
            send_row(rnd, level, True, solved.astype(bf16))
            sent_row(*before)
            before = (rnd, level, True)
            correction = correction + multiply(rnd, level, True, outer(level))
            rnd += 1
    rounded = forward.astype(bf16)
    start_value = rounded.astype(f32)

    def rs_copy(rnd, t):
        return pltpu.make_async_remote_copy(
            src_ref=rs_src.at[rnd, t], dst_ref=rs_buf.at[rnd, me],
            send_sem=rs_send.at[rnd], recv_sem=rs_recv.at[rnd],
            device_id=(t, col), device_id_type=MESH,
        )

    def backward_range(level, far):
        if far:
            first, active = lows[level], me >= lows[level - 1]
        else:
            first = jnp.maximum(lows[level], me - widest + 1)
            active = me <= highs[level]
        stop = jnp.minimum(me, highs[level] + 1)
        return first, jnp.where(active, jnp.maximum(stop, first), first)

    def scatter(rnd, level, far, value, masks):
        lo, hi = lows[level], highs[level]
        start, stop = backward_range(level, far)
        for first in range(lo, hi + 1, SPLIT):
            group = range(first, min(first + SPLIT, hi + 1))
            blocks = lax.dot_general(
                value, a_ref[:, group[0] * T:(group[-1] + 1) * T], NN_DIMS,
                preferred_element_type=f32,
            )
            for i, t in enumerate(group):
                rs_src[rnd, t] = jnp.where(
                    masks[t], blocks[:, i * T:(i + 1) * T], zeros
                ).astype(bf16)
            lax.fori_loop(
                jnp.maximum(start, group[0]), jnp.minimum(stop, group[-1] + 1),
                lambda t, x: (rs_copy(rnd, t).start(), x)[1], 0,
            )

    def scattered(rnd, level, far):
        start, stop = backward_range(level, far)
        settle(rs_send.at[rnd], stop - start, highs[level] + 1 - lows[level], True)

    def reduce(rnd, level, far, out):
        lo, hi = lows[level], highs[level]
        active = jnp.logical_and(me >= lo, me <= hi)
        if far:
            first, last = lows[level - 1], R - 1
        else:
            first, last = lo + 1, hi
        start = jnp.maximum(me + 1, first)
        stop = jnp.minimum(me + (R if far else widest - 1), last) + 1
        stop = jnp.where(active, jnp.maximum(stop, start), start)
        settle(rs_recv.at[rnd], stop - start, last + 1 - first, False)
        for k in range(first, last + 1):
            due = jnp.logical_and(start <= k, k < stop)
            out = out + jnp.where(due, rs_buf[rnd, k].astype(f32), zeros)
        return out

    def fin_copy(row):
        return pltpu.make_async_remote_copy(
            src_ref=fin_src, dst_ref=fin_buf.at[me // C, g],
            send_sem=fin_send, recv_sem=fin_recv,
            device_id=(row, lax.rem(me, C)), device_id_type=MESH,
        )

    own_copy = pltpu.make_async_copy(fin_src, fin_buf.at[me // C, g], own_sem)
    giver = lax.rem(me, C) // H == col // H
    local = lax.rem(me, C) == col

    def give(value):
        fin_src[...] = value.astype(bf16)

        def one(step, carry):
            fin_copy(lax.rem(me + step, R)).start()
            return carry

        lax.fori_loop(1, R, one, 0)

        @pl.when(local)
        def _():
            own_copy.start()

        @pl.when(jnp.logical_not(local))
        def _():
            fin_copy(me).start()

    def fwd_copy(j):
        return pltpu.make_async_remote_copy(
            src_ref=fwd_buf.at[g], dst_ref=fwd_buf.at[g],
            send_sem=fwd_send.at[j], recv_sem=fwd_recv.at[g],
            device_id=(me, base + lax.rem(g + j, H)), device_id_type=MESH,
        )

    answer = zeros
    current = rounded
    rnd = 0
    back = None
    for level in range(LEVELS):
        scatter(rnd, level, False, current, inner(level))
        if rnd == 0:
            sent_row(*before)
            fwd_buf[g] = forward
            for j in range(1, H):
                fwd_copy(j).start()
        if back is not None:
            scattered(*back)
        back = (rnd, level, False)
        solved = reduce(rnd, level, False, rs_src[rnd, me].astype(f32))
        answer = answer + jnp.where(row_level == level, solved, zeros)
        top = highs[level + 1] if level + 1 < LEVELS else -1
        ready = jnp.logical_and(me > top, me <= highs[level])

        @pl.when(jnp.logical_and(giver, ready))
        def _():
            give(answer)

        rnd += 1
        if level + 1 < LEVELS:
            scatter(rnd, level + 1, True, answer.astype(bf16), outer(level + 1))
            scattered(*back)
            back = (rnd, level + 1, True)
            current = (start_value - reduce(rnd, level + 1, True, zeros)).astype(bf16)
            rnd += 1
    scattered(*back)

    for step in range(1, C):
        raw_copy(step).wait_send()
    for j in range(1, H):
        fwd_copy(j).wait_send()
    for j in range(1, H):
        other = lax.rem(g + j, H)
        pltpu.make_async_remote_copy(
            src_ref=fwd_buf.at[g], dst_ref=fwd_buf.at[other],
            send_sem=fwd_send.at[j], recv_sem=fwd_recv.at[other],
            device_id=(me, base + other), device_id_type=MESH,
        ).wait_recv()
    for j in range(H):
        fwd_ref[j * Q:(j + 1) * Q, :] = fwd_buf[j]

    pl.when(local)(own_copy.wait)
    settle(fin_recv, CT * H - jnp.where(local, 1, 0), CT * H, False)
    for s in range(CT):
        for j in range(H):
            sol_ref[s, j * Q:(j + 1) * Q, :] = fin_buf[s, j]

    @pl.when(giver)
    def _():
        settle(fin_send, R - jnp.where(local, 1, 0), R, True)


def finish_kernel(rows_ref, tiles_ref, fwd_ref, sol_ref):
    fwd_ref[:, 0, :] = rows_ref[...]
    for s in range(tiles_ref.shape[0]):
        sol_ref[:, s, :] = tiles_ref[s].astype(jnp.float32)


def shards(R, C, right_sides, factor, node_sizes, row_blocks):
    rhs, row_tiles, T = right_sides.shape
    rows, CT = factor.shape[1], factor.shape[2]
    levels = (node_sizes.shape[0] + 1).bit_length() - 1
    assert row_tiles == 1 and rows == T and CT * C == R
    H = min(C, max(rhs // PACK, 1))
    assert C % H == 0 and rhs % H == 0
    Q = rhs // H
    rounds = 2 * levels - 1
    vmem = pl.BlockSpec(memory_space=pltpu.VMEM)
    dma = pltpu.SemaphoreType.DMA
    bf16, f32 = jnp.bfloat16, jnp.float32
    forward, tiles = pl.pallas_call(
        functools.partial(kernel, R, C, CT, levels, H),
        out_shape=(
            jax.ShapeDtypeStruct((rhs, T), f32),
            jax.ShapeDtypeStruct((CT, rhs, T), bf16),
        ),
        in_specs=[pl.BlockSpec(memory_space=pl.ANY)] * 4,
        out_specs=(vmem, vmem),
        scratch_shapes=[
            pltpu.SMEM(node_sizes.shape, jnp.int32),
            pltpu.SMEM(row_blocks.shape, jnp.int32),
            pltpu.VMEM(right_sides.shape, f32),
            pltpu.VMEM((C, rows, CT, T), bf16),
            pltpu.VMEM((T // LANES, CHUNK * CT, LANES), f32),
            pltpu.VMEM((rows, R * T), bf16),
            pltpu.VMEM((rounds, Q, T), bf16),
            pltpu.VMEM((rounds, R, Q, T), bf16),
            pltpu.VMEM((rounds, R, Q, T), bf16),
            pltpu.VMEM((rounds, R, Q, T), bf16),
            pltpu.VMEM((H, Q, T), f32),
            pltpu.VMEM((Q, T), bf16),
            pltpu.VMEM((CT, H, Q, T), bf16),
            dma((rounds,)),
            dma((rounds, pl.cdiv(R, GATHER))),
            dma((rounds,)),
            dma((rounds,)),
            dma((H,)),
            dma((H,)),
            dma,
            dma,
            dma,
            dma((C,)),
            dma((C,)),
            dma,
            dma((3,)),
        ],
        compiler_params=pltpu.CompilerParams(
            collective_id=0, has_side_effects=True, vmem_limit_bytes=GRANT
        ),
        name="tree_solve",
    )(*(
        pltpu.with_memory_space_constraint(x, pltpu.HBM)
        for x in (node_sizes, row_blocks, right_sides, factor)
    ))

    return pl.pallas_call(
        finish_kernel,
        out_shape=(
            jax.ShapeDtypeStruct((rhs, 1, T), f32),
            jax.ShapeDtypeStruct((rhs, CT, T), f32),
        ),
        in_specs=[vmem, vmem],
        out_specs=(vmem, vmem),
        compiler_params=pltpu.CompilerParams(vmem_limit_bytes=GRANT),
        name="place",
    )(forward, tiles)


def solution(mesh):
    in_specs = (P(None, None, "prow"), P(None, "prow", None, "pcol"), P(), P())
    out_specs = (P(None, None, "prow"), P(None, None, "pcol"))
    body = functools.partial(shards, mesh.shape["prow"], mesh.shape["pcol"])
    return jax.shard_map(
        body, mesh=mesh, in_specs=in_specs, out_specs=out_specs, check_vma=False
    )
```

```python
import functools

import jax
import jax.numpy as jnp
from jax import lax
from jax.experimental import pallas as pl
from jax.experimental.pallas import tpu as pltpu
from jax.sharding import PartitionSpec as P

MESH = pl.DeviceIdType.MESH
NT_DIMS = (((1,), (1,)), ((), ()))
NN_DIMS = (((1,), (0,)), ((), ()))
GATHER = 4
SPLIT = 8
CHUNK = 64
LANES = 128
PACK = 16
GRANT = 32 * 1024 * 1024


def kernel(
    R, C, CT, LEVELS, H,
    sizes_hbm, blocks_hbm, b_hbm, factor_ref,
    fwd_ref, sol_ref,
    sizes_ref, blocks_ref, b_ref,
    raw, wide, a_ref,
    ag_src, ag_buf, rs_src, rs_buf, fwd_buf, fin_src, fin_buf,
    ag_send, ag_recv, rs_send, rs_recv,
    fwd_send, fwd_recv, fin_send, fin_recv, own_sem, raw_send, raw_recv, load_sem, small_sem,
):
    SN = sizes_ref.shape[0]
    me = lax.axis_index("prow")
    col = lax.axis_index("pcol")
    base = (col // H) * H
    g = lax.rem(col, H)
    T = b_ref.shape[2]
    Q = b_ref.shape[0] // H
    f32, bf16 = jnp.float32, jnp.bfloat16

    widest = R - SN + 1
    lows, highs = [], []
    for level in range(LEVELS):
        first = SN - 1 - (2 ** (level + 1) - 2)
        last = SN - 1 - (2**level - 1)
        lows.append(first)
        highs.append(R - SN + last)

    load = pltpu.make_async_copy(factor_ref.at[0], raw.at[col], load_sem)
    small = [
        pltpu.make_async_copy(src, dst, small_sem.at[i])
        for i, (src, dst) in enumerate(
            ((sizes_hbm, sizes_ref), (blocks_hbm, blocks_ref), (b_hbm, b_ref))
        )
    ]
    for copy in small:
        copy.start()
    load.start()
    barrier = pltpu.get_barrier_semaphore()

    def greet(step, carry):
        row = lax.rem(me + R - 1 - step, R)
        for j in range(H):
            @pl.when(jnp.logical_or(step < R - 1, j > 0))
            def _():
                pl.semaphore_signal(
                    barrier, inc=1, device_id=(row, base + lax.rem(g + j, H)),
                    device_id_type=MESH,
                )
        return carry

    lax.fori_loop(0, R, greet, 0)

    def greet_row(step, carry):
        pl.semaphore_signal(
            barrier, inc=1, device_id=(me, lax.rem(base + H + step, C)),
            device_id_type=MESH,
        )
        return carry

    lax.fori_loop(0, C - H, greet_row, 0)

    for copy in small:
        copy.wait()
    ends = []
    total = jnp.int32(0)
    for s in range(SN):
        total = total + sizes_ref[s]
        ends.append(total)

    def node_of(tile):
        count = jnp.int32(0)
        for s in range(SN):
            count = count + jnp.where(ends[s] <= tile, 1, 0)
        return jnp.minimum(count, SN - 1)

    def level_of(label):
        level = jnp.int32(0)
        for e in range(1, LEVELS):
            level = level + jnp.where(label >= 2**e, 1, 0)
        return level

    row_node = node_of(me)
    row_label = SN - row_node
    row_level = level_of(row_label)
    same, linked, tile_level = [], [], []
    for k in range(R):
        node = node_of(k)
        label = SN - node
        above = jnp.int32(0)
        for gap in range(1, LEVELS):
            above = above + jnp.where(jnp.right_shift(label, gap) == row_label, 1, 0)
        flag = jnp.where(blocks_ref[node, me] == 1, 1, 0)
        low = jnp.where(k <= me, 1, 0)
        same.append(jnp.where(node == row_node, 1, 0) * low)
        linked.append(above * flag * low)
        tile_level.append(level_of(label))

    def inner(level):
        here = jnp.where(row_level == level, 1, 0)
        return [same[k] * here > 0 for k in range(R)]

    def outer(level):
        return [
            linked[k] * jnp.where(tile_level[k] == level, 1, 0) > 0 for k in range(R)
        ]

    b = b_ref[pl.ds(pl.multiple_of(g * Q, Q), Q), 0, :]
    zeros = jnp.zeros((Q, T), f32)

    def relayout(c):
        def body(step, carry):
            start = pl.multiple_of(step * CHUNK, CHUNK)
            rows = pl.ds(start, CHUNK)
            for h in range(T // LANES):
                block = raw[c, rows, :, h * LANES:(h + 1) * LANES].astype(f32)
                wide[h] = block.reshape(CHUNK * CT, LANES)
            for s in range(CT):
                for h in range(T // LANES):
                    part = wide[h, pl.ds(s, CHUNK, stride=CT), :]
                    at = pl.multiple_of((s * C + c) * T + h * LANES, LANES)
                    a_ref[rows, pl.ds(at, LANES)] = part.astype(bf16)
            return carry

        lax.fori_loop(0, T // CHUNK, body, 0)

    load.wait()
    relayout(col)
    pl.semaphore_wait(barrier, R * H - 1 + C - H)

    def raw_copy(step):
        return pltpu.make_async_remote_copy(
            src_ref=factor_ref.at[0], dst_ref=raw.at[col],
            send_sem=raw_send.at[step], recv_sem=raw_recv.at[col],
            device_id=(me, lax.rem(col + step, C)), device_id_type=MESH,
        )

    def raw_arrive(step, carry):
        origin = lax.rem(col + step, C)
        pltpu.make_async_remote_copy(
            src_ref=factor_ref.at[0], dst_ref=raw.at[origin],
            send_sem=raw_send.at[step], recv_sem=raw_recv.at[origin],
            device_id=(me, origin), device_id_type=MESH,
        ).wait_recv()
        relayout(origin)
        return carry

    def settle(sem, count, most, sent):
        for n in range(1, most + 1):
            done = pltpu.make_async_remote_copy(
                src_ref=rs_buf.at[0, 0:n], dst_ref=rs_buf.at[0, 0:n],
                send_sem=sem, recv_sem=sem, device_id=(me, col), device_id_type=MESH,
            )
            pl.when(count == n)(done.wait_send if sent else done.wait_recv)

    def ag_copy(rnd, k):
        return pltpu.make_async_remote_copy(
            src_ref=ag_src.at[rnd], dst_ref=ag_buf.at[rnd, me],
            send_sem=ag_send.at[rnd], recv_sem=ag_recv.at[rnd, me // GATHER],
            device_id=(k, col), device_id_type=MESH,
        )

    def forward_range(level, far):
        if far:
            first, last, reach = lows[level - 1], R - 1, R
        else:
            first, last, reach = lows[level], highs[level], widest - 1
        active = jnp.logical_and(me >= lows[level], me <= highs[level])
        start = jnp.maximum(me + 1, first)
        stop = jnp.minimum(me + reach, last) + 1
        return start, jnp.where(active, jnp.maximum(stop, start), start)

    def send_row(rnd, level, far, value):
        start, stop = forward_range(level, far)
        ag_src[rnd] = value
        lax.fori_loop(
            0, stop - start, lambda i, x: (ag_copy(rnd, start + i).start(), x)[1], 0
        )
        ag_buf[rnd, me] = value

    def sent_row(rnd, level, far):
        start, stop = forward_range(level, far)
        settle(ag_send.at[rnd], stop - start, R - 1, True)

    def multiply(rnd, level, far, masks):
        lo, hi = lows[level], highs[level]
        zero = jnp.zeros((Q, T), bf16)
        out = None
        for part in range(lo // GATHER, hi // GATHER + 1):
            last = min(part * GATHER + GATHER, hi + 1)
            group = range(max(part * GATHER, lo), last)
            if far:
                first, stop = group[0], jnp.minimum(me, last)
                due = me >= lows[level - 1]
            else:
                first, stop = jnp.maximum(group[0], me - widest + 1), jnp.minimum(me, last)
                due = me <= hi
            count = jnp.where(due, jnp.maximum(stop - first, 0), 0)
            settle(ag_recv.at[rnd, part], count, len(group), False)

            def add(acc, group=group):
                parts = [jnp.where(masks[k], ag_buf[rnd, k], zero) for k in group]
                return acc + lax.dot_general(
                    jnp.concatenate(parts, axis=1),
                    a_ref[:, group[0] * T:(group[-1] + 1) * T], NT_DIMS,
                    preferred_element_type=f32,
                )

            if out is None:
                out = add(jnp.zeros((Q, T), f32))
            else:
                out = lax.cond(group[0] <= me, add, lambda acc: acc, out)
        return out

    forward = zeros
    correction = zeros
    rnd = 0
    before = None
    for level in range(LEVELS - 1, -1, -1):
        send_row(rnd, level, False, (b - correction).astype(bf16))
        if rnd == 0:
            for step in range(1, C):
                raw_copy(step).start()
            lax.fori_loop(1, C, raw_arrive, 0)
        if before is not None:
            sent_row(*before)
        before = (rnd, level, False)
        solved = multiply(rnd, level, False, inner(level))
        solved = jnp.where(row_level == level, solved, zeros)
        forward = forward + solved
        rnd += 1
        if level > 0:
            send_row(rnd, level, True, solved.astype(bf16))
            sent_row(*before)
            before = (rnd, level, True)
            correction = correction + multiply(rnd, level, True, outer(level))
            rnd += 1
    rounded = forward.astype(bf16)
    start_value = rounded.astype(f32)

    def rs_copy(rnd, t):
        return pltpu.make_async_remote_copy(
            src_ref=rs_src.at[rnd, t], dst_ref=rs_buf.at[rnd, me],
            send_sem=rs_send.at[rnd], recv_sem=rs_recv.at[rnd],
            device_id=(t, col), device_id_type=MESH,
        )

    def backward_range(level, far):
        if far:
            first, active = lows[level], me >= lows[level - 1]
        else:
            first = jnp.maximum(lows[level], me - widest + 1)
            active = me <= highs[level]
        stop = jnp.minimum(me, highs[level] + 1)
        return first, jnp.where(active, jnp.maximum(stop, first), first)

    def scatter(rnd, level, far, value, masks):
        lo, hi = lows[level], highs[level]
        start, stop = backward_range(level, far)
        for part in range(hi // SPLIT, lo // SPLIT - 1, -1):
            group = range(max(part * SPLIT, lo), min(part * SPLIT + SPLIT, hi + 1))

            @pl.when(group[0] <= me)
            def _(group=group):
                blocks = lax.dot_general(
                    value, a_ref[:, group[0] * T:(group[-1] + 1) * T], NN_DIMS,
                    preferred_element_type=f32,
                )
                for i, t in enumerate(group):
                    rs_src[rnd, t] = jnp.where(
                        masks[t], blocks[:, i * T:(i + 1) * T], zeros
                    ).astype(bf16)

            lax.fori_loop(
                jnp.maximum(start, group[0]), jnp.minimum(stop, group[-1] + 1),
                lambda t, x, a=group[0], z=group[-1] + 1: (rs_copy(rnd, jnp.maximum(start, a) + jnp.minimum(stop, z) - 1 - t).start(), x)[1], 0,
            )

    def scattered(rnd, level, far):
        start, stop = backward_range(level, far)
        settle(rs_send.at[rnd], stop - start, highs[level] + 1 - lows[level], True)

    def reduce(rnd, level, far, out):
        lo, hi = lows[level], highs[level]
        active = jnp.logical_and(me >= lo, me <= hi)
        if far:
            first, last = lows[level - 1], R - 1
        else:
            first, last = lo + 1, hi
        start = jnp.maximum(me + 1, first)
        stop = jnp.minimum(me + (R if far else widest - 1), last) + 1
        stop = jnp.where(active, jnp.maximum(stop, start), start)
        settle(rs_recv.at[rnd], stop - start, last + 1 - first, False)
        for k in range(first, last + 1):
            due = jnp.logical_and(start <= k, k < stop)
            out = out + jnp.where(due, rs_buf[rnd, k].astype(f32), zeros)
        return out

    def fin_copy(row):
        return pltpu.make_async_remote_copy(
            src_ref=fin_src, dst_ref=fin_buf.at[me // C, g],
            send_sem=fin_send, recv_sem=fin_recv,
            device_id=(row, lax.rem(me, C)), device_id_type=MESH,
        )

    own_copy = pltpu.make_async_copy(fin_src, fin_buf.at[me // C, g], own_sem)
    giver = lax.rem(me, C) // H == col // H
    local = lax.rem(me, C) == col

    def give(value):
        fin_src[...] = value.astype(bf16)

        def one(step, carry):
            fin_copy(lax.rem(me + step, R)).start()
            return carry

        lax.fori_loop(1, R, one, 0)

        @pl.when(local)
        def _():
            own_copy.start()

        @pl.when(jnp.logical_not(local))
        def _():
            fin_copy(me).start()

    def fwd_copy(j):
        return pltpu.make_async_remote_copy(
            src_ref=fwd_buf.at[g], dst_ref=fwd_buf.at[g],
            send_sem=fwd_send.at[j], recv_sem=fwd_recv.at[g],
            device_id=(me, base + lax.rem(g + j, H)), device_id_type=MESH,
        )

    answer = zeros
    current = rounded
    rnd = 0
    back = None
    for level in range(LEVELS):
        scatter(rnd, level, False, current, inner(level))
        if rnd == 0:
            sent_row(*before)
            fwd_buf[g] = forward
            for j in range(1, H):
                fwd_copy(j).start()
        if back is not None:
            scattered(*back)
        back = (rnd, level, False)
        solved = reduce(rnd, level, False, rs_src[rnd, me].astype(f32))
        answer = answer + jnp.where(row_level == level, solved, zeros)
        top = highs[level + 1] if level + 1 < LEVELS else -1
        ready = jnp.logical_and(me > top, me <= highs[level])

        @pl.when(jnp.logical_and(giver, ready))
        def _():
            give(answer)

        rnd += 1
        if level + 1 < LEVELS:
            scatter(rnd, level + 1, True, answer.astype(bf16), outer(level + 1))
            scattered(*back)
            back = (rnd, level + 1, True)
            current = (start_value - reduce(rnd, level + 1, True, zeros)).astype(bf16)
            rnd += 1
    scattered(*back)

    for step in range(1, C):
        raw_copy(step).wait_send()
    for j in range(1, H):
        fwd_copy(j).wait_send()
    for j in range(1, H):
        other = lax.rem(g + j, H)
        pltpu.make_async_remote_copy(
            src_ref=fwd_buf.at[g], dst_ref=fwd_buf.at[other],
            send_sem=fwd_send.at[j], recv_sem=fwd_recv.at[other],
            device_id=(me, base + other), device_id_type=MESH,
        ).wait_recv()
    for j in range(H):
        fwd_ref[j * Q:(j + 1) * Q, :] = fwd_buf[j]

    pl.when(local)(own_copy.wait)
    settle(fin_recv, CT * H - jnp.where(local, 1, 0), CT * H, False)
    for s in range(CT):
        for j in range(H):
            sol_ref[s, j * Q:(j + 1) * Q, :] = fin_buf[s, j]

    @pl.when(giver)
    def _():
        settle(fin_send, R - jnp.where(local, 1, 0), R, True)


def finish_kernel(rows_ref, tiles_ref, fwd_ref, sol_ref):
    fwd_ref[:, 0, :] = rows_ref[...]
    for s in range(tiles_ref.shape[0]):
        sol_ref[:, s, :] = tiles_ref[s].astype(jnp.float32)


def shards(R, C, right_sides, factor, node_sizes, row_blocks):
    rhs, row_tiles, T = right_sides.shape
    rows, CT = factor.shape[1], factor.shape[2]
    levels = (node_sizes.shape[0] + 1).bit_length() - 1
    assert row_tiles == 1 and rows == T and CT * C == R
    H = min(C, max(rhs // PACK, 1))
    assert C % H == 0 and rhs % H == 0
    Q = rhs // H
    rounds = 2 * levels - 1
    vmem = pl.BlockSpec(memory_space=pltpu.VMEM)
    dma = pltpu.SemaphoreType.DMA
    bf16, f32 = jnp.bfloat16, jnp.float32
    forward, tiles = pl.pallas_call(
        functools.partial(kernel, R, C, CT, levels, H),
        out_shape=(
            jax.ShapeDtypeStruct((rhs, T), f32),
            jax.ShapeDtypeStruct((CT, rhs, T), bf16),
        ),
        in_specs=[pl.BlockSpec(memory_space=pl.ANY)] * 4,
        out_specs=(vmem, vmem),
        scratch_shapes=[
            pltpu.SMEM(node_sizes.shape, jnp.int32),
            pltpu.SMEM(row_blocks.shape, jnp.int32),
            pltpu.VMEM(right_sides.shape, f32),
            pltpu.VMEM((C, rows, CT, T), bf16),
            pltpu.VMEM((T // LANES, CHUNK * CT, LANES), f32),
            pltpu.VMEM((rows, R * T), bf16),
            pltpu.VMEM((rounds, Q, T), bf16),
            pltpu.VMEM((rounds, R, Q, T), bf16),
            pltpu.VMEM((rounds, R, Q, T), bf16),
            pltpu.VMEM((rounds, R, Q, T), bf16),
            pltpu.VMEM((H, Q, T), f32),
            pltpu.VMEM((Q, T), bf16),
            pltpu.VMEM((CT, H, Q, T), bf16),
            dma((rounds,)),
            dma((rounds, pl.cdiv(R, GATHER))),
            dma((rounds,)),
            dma((rounds,)),
            dma((H,)),
            dma((H,)),
            dma,
            dma,
            dma,
            dma((C,)),
            dma((C,)),
            dma,
            dma((3,)),
        ],
        compiler_params=pltpu.CompilerParams(
            collective_id=0, has_side_effects=True, vmem_limit_bytes=GRANT
        ),
        name="tree_solve",
    )(*(
        pltpu.with_memory_space_constraint(x, pltpu.HBM)
        for x in (node_sizes, row_blocks, right_sides, factor)
    ))

    return pl.pallas_call(
        finish_kernel,
        out_shape=(
            jax.ShapeDtypeStruct((rhs, 1, T), f32),
            jax.ShapeDtypeStruct((rhs, CT, T), f32),
        ),
        in_specs=[vmem, vmem],
        out_specs=(vmem, vmem),
        compiler_params=pltpu.CompilerParams(vmem_limit_bytes=GRANT),
        name="place",
    )(forward, tiles)


def solution(mesh):
    in_specs = (P(None, None, "prow"), P(None, "prow", None, "pcol"), P(), P())
    out_specs = (P(None, None, "prow"), P(None, None, "pcol"))
    body = functools.partial(shards, mesh.shape["prow"], mesh.shape["pcol"])
    return jax.shard_map(
        body, mesh=mesh, in_specs=in_specs, out_specs=out_specs, check_vma=False
    )
```
